32 devices in a mesh: dp: 16 (over z, x, core), mp: 2 (over y).
Axes of the slice: x: 2, y: 2, z: 4, core: 2. Of those that a mesh axis runs over, the one named last changes fastest.
Arguments:
- hidden_in: bfloat16 [16384, 1024], P(('dp', 'mp')), may hold values from -6 to 6
- lengths: int32 [32], P('dp'), may hold values from 80 to 512, as said below
- key_mask: int32 [32, 512], P('dp'), may hold values from 0 to 1, as said below
- w_qkv: bfloat16 [1024, 3, 1024], P(None, None, 'mp'), may hold values from -0.1875 to 0.1875
- b_qv: bfloat16 [2, 1024], P(None, 'mp'), may hold values from -3 to 3
- w_out: bfloat16 [1024, 1024], P('mp'), may hold values from -1.5 to 1.5
- b_out: bfloat16 [1024], replicated, may hold values from -3 to 3
- ln1_gain: bfloat16 [1024], replicated, may hold values from 0.5 to 1.5
- ln1_bias: bfloat16 [1024], replicated, may hold values from -3 to 3
- w_up: bfloat16 [1024, 4096], P(None, 'mp'), may hold values from -0.1875 to 0.1875
- b_up: bfloat16 [4096], P('mp'), may hold values from -3 to 3
- w_down: bfloat16 [4096, 1024], P('mp'), may hold values from -0.09375 to 0.09375
- b_down: bfloat16 [1024], replicated, may hold values from -3 to 3
- ln2_gain: bfloat16 [1024], replicated, may hold values from 0.5 to 1.5
- ln2_bias: bfloat16 [1024], replicated, may hold values from -3 to 3
- out_cotangent: bfloat16 [16384, 1024], P(('dp', 'mp')), may hold values from -6 to 6
Outputs:
- layer_out: float32 [16384, 1024], P(('dp', 'mp'))
- input_grad: float32 [16384, 1024], P(('dp', 'mp'))
- w_qkv_grad: float32 [1024, 3, 1024], P(None, None, 'mp')
- b_qv_grad: float32 [2, 1024], P(None, 'mp')
- w_out_grad: float32 [1024, 1024], P('mp')
- b_out_grad: float32 [1024], replicated
- ln1_gain_grad: float32 [1024], replicated
- ln1_bias_grad: float32 [1024], replicated
- w_up_grad: float32 [1024, 4096], P(None, 'mp')
- b_up_grad: float32 [4096], P('mp')
- w_down_grad: float32 [4096, 1024], P('mp')
- b_down_grad: float32 [1024], replicated
- ln2_gain_grad: float32 [1024], replicated
- ln2_bias_grad: float32 [1024], replicated
The draws below stay inside these ranges and needn't reach their ends.
Inputs may be any that keep to these rules, and one draw needn't show every extreme that they name: `lengths`: some page has 512 real tokens and some page has 80. `key_mask`: slot 0 of every page is 1.
All inputs are finite; a program needn't handle non-finite values.
Results may differ from the reference program's by a relative error of at most 0.02.
Values may be sent and summed in bfloat16 or wider, within the bound.
No kernel may reach another device: no remote copies, remote signals or barrier semaphores. Data moves between devices by JAX's collectives and lax.ppermute only.
A program may use at most 192 MiB of HBM per device.

```python
import math
import jax
import jax.numpy as jnp
from jax import lax

D = 1024
HEADS = 16
HD = 64
FF = 4096
PAGE = 512
MIN_LEN = 80
PAGES = 32
TOKENS = 16384


def draw_lengths(key, part):
    base = jax.random.randint(jax.random.fold_in(key, 11), (PAGES,), MIN_LEN, PAGE + 1, dtype=jnp.int32)
    full_page = jax.random.randint(jax.random.fold_in(key, 12), (), 0, PAGES, dtype=jnp.int32)
    index = jnp.arange(PAGES, dtype=jnp.int32)
    base = jnp.where(index == full_page, PAGE, base)
    base = jnp.where(index == (full_page + 1) % PAGES, MIN_LEN, base)
    return base


def draw_key_mask(key, part):
    bits = jax.random.randint(jax.random.fold_in(key, 13), (PAGES, PAGE), 0, 4, dtype=jnp.int32)
    opened = (bits != 0).astype(jnp.int32)
    column = jnp.arange(PAGE, dtype=jnp.int32)[None, :]
    return jnp.where(column == 0, 1, opened)


def levels(stream_key, dims, shards, least, largest):
    loudness, own = 1.0, jax.random.fold_in(stream_key, 6)
    for dim, shards_of in shards:
        steps = jnp.exp(jax.random.uniform(jax.random.fold_in(own, dim), (shards_of,), jnp.float32, least / len(shards), largest / len(shards)))
        loudness = loudness * jnp.repeat(steps, dims[dim] // shards_of).reshape([-1 if axis == dim else 1 for axis in range(len(dims))])
    return loudness


def gaussian(stream_key, dims, width, limit, pieces=(), kind=jnp.bfloat16):
    result = width * jax.random.normal(stream_key, dims, jnp.float32)
    if pieces:
        result = result * levels(stream_key, dims, pieces, -0.22, 0.18)
    return jnp.clip(result, -limit, limit).astype(kind)


def setup_inputs(seed: int = 0) -> dict:
    seeds = jax.random.split(jax.random.key(seed), 17)
    hidden_in = gaussian(seeds[0], (TOKENS, D), 1.0, 6.0, ((0, 32),))
    lengths = draw_lengths(jax.random.fold_in(seeds[16], 71), 0)
    key_mask = draw_key_mask(jax.random.fold_in(seeds[16], 71), 0)
    w_qkv = gaussian(seeds[3], (D, 3, D), D ** -0.5, 0.1875, ((2, 2),))
    b_qv = gaussian(seeds[4], (2, D), 0.5, 3.0, ((1, 2),))
    w_out = gaussian(seeds[5], (D, D), (D // 64) ** -0.5, 1.5, ((0, 2),))
    b_out = gaussian(seeds[6], (D,), 0.5, 3.0)
    ln1_gain = jnp.clip(1.0 + 0.1 * jax.random.normal(seeds[7], (D,), jnp.float32), 0.5, 1.5).astype(jnp.bfloat16)
    ln1_bias = gaussian(seeds[8], (D,), 0.5, 3.0)
    w_up = gaussian(seeds[9], (D, FF), D ** -0.5, 0.1875, ((1, 2),))
    b_up = gaussian(seeds[10], (FF,), 0.5, 3.0, ((0, 2),))
    w_down = gaussian(seeds[11], (FF, D), FF ** -0.5, 0.09375, ((0, 2),))
    b_down = gaussian(seeds[12], (D,), 0.5, 3.0)
    ln2_gain = jnp.clip(1.0 + 0.1 * jax.random.normal(seeds[13], (D,), jnp.float32), 0.5, 1.5).astype(jnp.bfloat16)
    ln2_bias = gaussian(seeds[14], (D,), 0.5, 3.0)
    out_cotangent = gaussian(seeds[15], (TOKENS, D), 1.0, 6.0, ((0, 32),))
    return dict(hidden_in=hidden_in, lengths=lengths, key_mask=key_mask, w_qkv=w_qkv, b_qv=b_qv, w_out=w_out, b_out=b_out, ln1_gain=ln1_gain, ln1_bias=ln1_bias, w_up=w_up, b_up=b_up, w_down=w_down, b_down=b_down, ln2_gain=ln2_gain, ln2_bias=ln2_bias, out_cotangent=out_cotangent)


EPS = 1e-12
MASKED_SCORE = -1e+30
EXACT = lax.Precision.HIGHEST

@jax.custom_vjp
def low(v):
    return lax.optimization_barrier(v.astype(jnp.bfloat16)).astype(jnp.float32)

@jax.custom_vjp
def low_back(v):
    return v

def low_keep(v):
    return (low(v), None)

def low_pass(kept, grad):
    return (grad,)

def back_keep(v):
    return (v, None)

def back_low(kept, grad):
    return (low(grad),)
low.defvjp(low_keep, low_pass)
low_back.defvjp(back_keep, back_low)

def layer_norm(resid, gain, bias):
    center = resid - lax.optimization_barrier(jnp.mean(resid, axis=-1, keepdims=True))
    spread = lax.optimization_barrier(jnp.mean(center * center, axis=-1, keepdims=True))
    return center * lax.rsqrt(spread + EPS) * gain + bias

def page_attention(inputs):
    projected, valid = inputs
    heads = projected.reshape(PAGE, 3, HEADS, HD)
    query = heads[:, 0]
    keys = heads[:, 1]
    values = heads[:, 2]
    scores = jnp.einsum('qhd,khd->hqk', query, keys, precision=EXACT) * float(HD) ** (-0.5)
    scores = low_back(scores)
    scores = jnp.where(valid[None, None, :], scores, MASKED_SCORE)
    highest = lax.optimization_barrier(jnp.max(scores, axis=-1, keepdims=True))
    expo = jnp.exp(scores - highest)
    probs = expo / lax.optimization_barrier(jnp.sum(expo, axis=-1, keepdims=True))
    context = jnp.einsum('hqk,khd->qhd', low(probs), values, precision=EXACT)
    return context.reshape(PAGE, HEADS * HD)

def forward_block(params, inputs, valid):
    w_qkv, b_qv, w_out, b_out, ln1_gain, ln1_bias, w_up, b_up, w_down, b_down, ln2_gain, ln2_bias = params
    bias_rows = jnp.stack([b_qv[0], jnp.zeros_like(b_qv[0]), b_qv[1]])
    projected = jnp.einsum('td,dce->tce', inputs, w_qkv, precision=EXACT) + bias_rows
    projected = low(low_back(projected))
    block_pages = valid.shape[0]
    context = lax.map(jax.checkpoint(page_attention), (projected.reshape(block_pages, PAGE, 3 * D), valid))
    context = low(low_back(context.reshape(block_pages * PAGE, D)))
    attn_branch = low_back(jnp.dot(context, w_out, precision=EXACT) + b_out)
    normed1 = layer_norm(inputs + attn_branch, ln1_gain, ln1_bias)
    up_linear = low_back(jnp.dot(low(normed1), w_up, precision=EXACT) + b_up)
    up_active = low(jax.nn.gelu(up_linear, approximate=False))
    ffn_branch = low_back(jnp.dot(up_active, w_down, precision=EXACT) + b_down)
    return layer_norm(normed1 + ffn_branch, ln2_gain, ln2_bias)

def reference(hidden_in, lengths, key_mask, w_qkv, b_qv, w_out, b_out, ln1_gain, ln1_bias, w_up, b_up, w_down, b_down, ln2_gain, ln2_bias, out_cotangent):
    params = tuple((weight.astype(jnp.float32) for weight in (w_qkv, b_qv, w_out, b_out, ln1_gain, ln1_bias, w_up, b_up, w_down, b_down, ln2_gain, ln2_bias)))
    slots = jnp.arange(PAGE, dtype=jnp.int32)
    below = slots[None, :] < lengths[:, None]
    valid = below & (key_mask == 1)
    live = below.astype(jnp.float32).reshape(TOKENS, 1)
    block_pages = math.gcd(PAGES, 8)
    blocks = PAGES // block_pages
    inputs = hidden_in.astype(jnp.float32).reshape(blocks, block_pages * PAGE, D)
    cotangent = (out_cotangent.astype(jnp.float32) * live).reshape(blocks, block_pages * PAGE, D)
    valid_blocks = valid.reshape(blocks, block_pages, PAGE)

    def one_block(totals, block):
        block_in, block_valid, block_cot = block

        def forward_here(weights_in, rows_in):
            return forward_block(weights_in, rows_in, block_valid)
        block_out, pull = jax.vjp(forward_here, params, block_in)
        param_grads, row_grads = pull(block_cot)
        totals = jax.tree.map(lambda total, grad: total + grad, totals, param_grads)
        return (totals, (block_out, row_grads))
    start_totals = jax.tree.map(jnp.zeros_like, params)
    totals, (layer_out, input_grad) = lax.scan(one_block, start_totals, (inputs, valid_blocks, cotangent))
    return (layer_out.reshape(TOKENS, D), input_grad.reshape(TOKENS, D), totals[0], totals[1], totals[2], totals[3], totals[4], totals[5], totals[6], totals[7], totals[8], totals[9], totals[10], totals[11])
```

```python
import math

import jax
import jax.numpy as jnp
from jax import lax
from jax.experimental import pallas as pl
from jax.experimental.pallas import tpu as pltpu
from jax.sharding import PartitionSpec as P

HD = 64
PAGE = 512


EPS = 1e-12
MASKED_SCORE = -1e30


def layer_norm_parts(resid, gain, bias):
    center = resid - jnp.mean(resid, axis=-1, keepdims=True)
    spread = jnp.mean(center * center, axis=-1, keepdims=True)
    inv_scale = lax.rsqrt(spread + EPS)
    unit_rows = center * inv_scale
    return (unit_rows * gain + bias, unit_rows, inv_scale)


def layer_norm_back(incoming, unit_rows, inv_scale, gain):
    scaled = incoming * gain
    inner = (
        scaled
        - jnp.mean(scaled, axis=-1, keepdims=True)
        - unit_rows * jnp.mean(scaled * unit_rows, axis=-1, keepdims=True)
    )
    return (inv_scale * inner, jnp.sum(incoming * unit_rows, axis=0), jnp.sum(incoming, axis=0))


def page_scores(query, keys, valid, factor):
    scores = jnp.einsum("pqhd,pkhd->phqk", query, keys, preferred_element_type=jnp.float32) * factor
    return jnp.where(valid[:, None, None, :], scores, MASKED_SCORE)


def gelu_exact(linear):
    return jax.nn.gelu(linear, approximate=False)


def cut(value, index, parts, axis):
    size = value.shape[axis] // parts
    return lax.dynamic_slice_in_dim(value, index * size, size, axis)


def ordered(first, mine, other, axis):
    return jnp.where(
        first,
        jnp.concatenate([mine, other], axis=axis),
        jnp.concatenate([other, mine], axis=axis),
    )


def dot_nn(a, b):
    return lax.dot_general(a, b, (((1,), (0,)), ((), ())), preferred_element_type=jnp.float32)


def dot_nt(a, b):
    return lax.dot_general(a, b, (((1,), (1,)), ((), ())), preferred_element_type=jnp.float32)


def dot_tn(a, b):
    return lax.dot_general(a, b, (((0,), (0,)), ((), ())), preferred_element_type=jnp.float32)


def wide(value):
    return value.astype(jnp.float32)


def low(value):
    return value.astype(jnp.bfloat16)


LOG2E = 1.4426950408889634
ANYWHERE = pl.BlockSpec(memory_space=pl.ANY)


def head_lanes(value, head):
    lane = lax.broadcasted_iota(jnp.int32, value.shape, 1)
    return jnp.where((lane // HD) == head, value, jnp.zeros_like(value))


def attend_kernel(parts, *refs):
    rows = [ref[...] for ref in refs[:parts]]
    weights = refs[parts : 2 * parts]
    mask_ref, bias_ref = refs[2 * parts : 2 * parts + 2]
    qkv_ref, context_ref, lse_ref = refs[-3:]
    scale = float(HD) ** (-0.5) * LOG2E
    bias = wide(bias_ref[...])

    def project(c):
        total = dot_nn(rows[0], weights[0][c])
        for i in range(1, parts):
            total = total + dot_nn(rows[i], weights[i][c])
        return total

    query = low(project(0) + bias[0:1])
    keys = low(project(1))
    values = low(project(2) + bias[1:2])
    qkv_ref[0] = query
    qkv_ref[1] = keys
    qkv_ref[2] = values
    mask = mask_ref[0]
    total = None
    for head in range(2):
        scores = dot_nt(keys, head_lanes(query, head)) + mask
        highest = jnp.max(scores, axis=0, keepdims=True) * scale
        expo = jnp.exp2(scores * scale - highest)
        expo_sum = jnp.sum(expo, axis=0, keepdims=True)
        probs = low(expo * (1.0 / expo_sum))
        part = dot_tn(head_lanes(values, head), probs)
        total = part if total is None else total + part
        lse_ref[0, head : head + 1, :] = highest + jnp.log2(expo_sum)
    context_ref[...] = low(total.T)


def attend(rows, mask, weights, bias, pairs_all, first, into, name):
    parts = len(rows)
    tokens = rows[0].shape[0]
    pages = tokens // PAGE
    pairs = weights[0].shape[2] // (2 * HD)
    local = pairs_all * 2 * HD
    in_specs = (
        [pl.BlockSpec((PAGE, r.shape[1]), lambda p, h: (p, 0)) for r in rows]
        + [pl.BlockSpec((3, w.shape[1], 2 * HD), lambda p, h: (0, 0, h)) for w in weights]
        + [
            pl.BlockSpec((1, PAGE, 1), lambda p, h: (p, 0, 0)),
            pl.BlockSpec((2, 2 * HD), lambda p, h: (0, h)),
        ]
    )
    args = [*rows, *weights, mask, bias]
    aliases = {}
    if into is not None:
        aliases = {len(args) + i: i for i in range(3)}
        in_specs += [ANYWHERE] * 3
        args += list(into)

    def kernel(*refs):
        attend_kernel(parts, *refs)

    return pl.pallas_call(
        kernel,
        grid=(pages, pairs),
        in_specs=in_specs,
        out_specs=[
            pl.BlockSpec((3, PAGE, 2 * HD), lambda p, h: (0, p, h + first)),
            pl.BlockSpec((PAGE, 2 * HD), lambda p, h: (p, h + first)),
            pl.BlockSpec((1, 2, PAGE), lambda p, h: (h + first, 0, p)),
        ],
        out_shape=[
            jax.ShapeDtypeStruct((3, tokens, local), jnp.bfloat16),
            jax.ShapeDtypeStruct((tokens, local), jnp.bfloat16),
            jax.ShapeDtypeStruct((pairs_all, 2, tokens), jnp.float32),
        ],
        input_output_aliases=aliases,
        name=name,
    )(*args)


def attend_back_kernel(parts, *refs):
    grads = [ref[...] for ref in refs[:parts]]
    weights = refs[parts : 2 * parts]
    mask_ref, qkv_ref, lse_ref, dqkv_ref, sums_ref = refs[2 * parts :]
    factor = float(HD) ** (-0.5)
    scale = factor * LOG2E
    context_grad = dot_nt(grads[0], weights[0][...])
    for i in range(1, parts):
        context_grad = context_grad + dot_nt(grads[i], weights[i][...])
    context_grad = low(context_grad)
    query, keys, values = qkv_ref[0], qkv_ref[1], qkv_ref[2]
    mask = mask_ref[0]
    dq = dk = dv = None
    for head in range(2):
        query_one = head_lanes(query, head)
        grad_one = head_lanes(context_grad, head)
        scores = dot_nt(keys, query_one) + mask
        probs = jnp.exp2(scores * scale - lse_ref[0, head : head + 1, :])
        prob_grad = dot_nt(values, grad_one)
        inner = jnp.sum(probs * prob_grad, axis=0, keepdims=True)
        score_grad = low(probs * (prob_grad - inner))
        dq_one = dot_tn(head_lanes(keys, head), score_grad)
        dk_one = dot_nn(score_grad, query_one)
        dv_one = dot_nn(low(probs), grad_one)
        dq = dq_one if dq is None else dq + dq_one
        dk = dk_one if dk is None else dk + dk_one
        dv = dv_one if dv is None else dv + dv_one
    dq_low = low(dq.T * factor)
    dv_low = low(dv)
    dqkv_ref[0] = dq_low
    dqkv_ref[1] = low(dk * factor)
    dqkv_ref[2] = dv_low
    sums_ref[0, 0:1, :] = jnp.sum(wide(dq_low), axis=0, keepdims=True)
    sums_ref[0, 1:2, :] = jnp.sum(wide(dv_low), axis=0, keepdims=True)


def attend_back(grads, mask, w_out, qkv, lse, name):
    parts = len(grads)
    tokens = grads[0].shape[0]
    pages = tokens // PAGE
    local = qkv.shape[2]
    pairs = local // (2 * HD)

    def kernel(*refs):
        attend_back_kernel(parts, *refs)

    return pl.pallas_call(
        kernel,
        grid=(pages, pairs),
        in_specs=[pl.BlockSpec((PAGE, g.shape[1]), lambda p, h: (p, 0)) for g in grads]
        + [pl.BlockSpec((2 * HD, w.shape[1]), lambda p, h: (h, 0)) for w in w_out]
        + [
            pl.BlockSpec((1, PAGE, 1), lambda p, h: (p, 0, 0)),
            pl.BlockSpec((3, PAGE, 2 * HD), lambda p, h: (0, p, h)),
            pl.BlockSpec((1, 2, PAGE), lambda p, h: (h, 0, p)),
        ],
        out_specs=[
            pl.BlockSpec((3, PAGE, 2 * HD), lambda p, h: (0, p, h)),
            pl.BlockSpec((1, 2, 2 * HD), lambda p, h: (p, 0, h)),
        ],
        out_shape=[
            jax.ShapeDtypeStruct((3, tokens, local), jnp.bfloat16),
            jax.ShapeDtypeStruct((pages, 2, local), jnp.float32),
        ],
        name=name,
    )(*grads, *w_out, mask, qkv, lse)


def up_kernel(parts, *refs):
    bias_ref = refs[2 * parts]
    active_ref, slope_ref = refs[-2:]
    linear = dot_nn(refs[0][...], refs[parts][...])
    for i in range(1, parts):
        linear = linear + dot_nn(refs[i][...], refs[parts + i][...])
    linear = linear + wide(bias_ref[...])
    share = 0.5 * (1.0 + lax.erf(linear * (0.5**0.5)))
    active_ref[...] = low(linear * share)
    density = jnp.exp(-0.5 * linear * linear) * ((0.5 / math.pi) ** 0.5)
    slope_ref[...] = low(share + linear * density)


def up_and_gelu(rows, weights, bias, units_all, first, into, name):
    parts = len(rows)
    tokens = rows[0].shape[0]
    units = weights[0].shape[1]
    tile = math.gcd(units, 512)
    out = jax.ShapeDtypeStruct((tokens, units_all), jnp.bfloat16)
    in_specs = (
        [pl.BlockSpec((PAGE, r.shape[1]), lambda p, n: (p, 0)) for r in rows]
        + [pl.BlockSpec((w.shape[0], tile), lambda p, n: (0, n)) for w in weights]
        + [pl.BlockSpec((1, tile), lambda p, n: (0, n))]
    )
    args = [*rows, *weights, bias.reshape(1, units)]
    aliases = {}
    if into is not None:
        aliases = {len(args) + i: i for i in range(2)}
        in_specs += [ANYWHERE] * 2
        args += list(into)
    skip = first // tile

    def kernel(*refs):
        up_kernel(parts, *refs)

    return pl.pallas_call(
        kernel,
        grid=(tokens // PAGE, units // tile),
        in_specs=in_specs,
        out_specs=[pl.BlockSpec((PAGE, tile), lambda p, n: (p, n + skip))] * 2,
        out_shape=[out, out],
        input_output_aliases=aliases,
        name=name,
    )(*args)


def after(value, earlier):
    return lax.optimization_barrier((value, earlier))[0]


def paged(
    hidden_in, lengths, key_mask, w_qkv, b_qv, w_out, b_out, ln1_gain, ln1_bias, w_up, b_up,
    w_down, b_down, ln2_gain, ln2_bias, out_cotangent, dp,
):
    rows, width = hidden_in.shape
    local = w_qkv.shape[2]
    units = w_up.shape[1]
    pages = rows // PAGE
    y = lax.axis_index("mp")
    place_dp = lax.axis_index("dp")
    core = place_dp % 2
    x = (place_dp // 2) % 2
    near = (place_dp // 4) % 2

    def mover(axis, bit, size, tail):
        pairs = [(i, i ^ bit) for i in range(size)]

        def move(value, name):
            with jax.named_scope(name + tail):
                return lax.ppermute(value, axis, pairs)

        return move

    over_core = mover("dp", 1, dp, "_core")
    over_x = mover("dp", 2, dp, "_x")
    over_near = mover("dp", 4, dp, "_near")
    over_far = mover("dp", 8, dp, "_far")
    over_y = mover("mp", 1, 2, "_y")

    def halves(value):
        return [cut(value, core, 2, 1), cut(value, 1 - core, 2, 1)]

    w_three = jnp.transpose(w_qkv, (1, 0, 2))
    small_peer = over_y(jnp.concatenate([b_qv.reshape(-1), b_up]), "small")
    b_qv_peer = small_peer[: 2 * local].reshape(2, local)
    b_up_peer = small_peer[2 * local :]

    def quarter(value, unit_axis, feature_axis):
        return cut(cut(value, x, 2, unit_axis), core, 2, feature_axis)

    def spread(first, name):
        side = over_x(first, name)
        return [first, over_core(first, name)], [side, over_core(side, name + "_side")]

    qkv_first = over_y(quarter(w_three, 2, 1), "wqkv")
    up_first = over_y(after(quarter(w_up, 1, 0), qkv_first), "wup")
    out_first = over_y(after(quarter(w_out, 0, 1), qkv_first), "wout")
    down_first = over_y(after(quarter(w_down, 0, 1), up_first), "wdown")
    qkv_near, qkv_side = spread(qkv_first, "wqkv")
    out_near, out_side = spread(out_first, "wout")
    up_near, up_side = spread(up_first, "wup")
    down_near, down_side = spread(down_first, "wdown")
    w_out_peer = [jnp.concatenate([a, b], axis=0) for a, b in zip(out_near, out_side)]
    w_down_peer = [jnp.concatenate([a, b], axis=0) for a, b in zip(down_near, down_side)]

    my_lengths = lax.dynamic_slice_in_dim(lengths, y * pages, pages, 0)
    my_mask = lax.dynamic_slice_in_dim(key_mask, y * pages, pages, 0)
    slots = jnp.arange(PAGE, dtype=jnp.int32)
    below = slots[None, :] < my_lengths[:, None]
    mask = jnp.where(below & (my_mask == 1), 0.0, MASKED_SCORE)[:, :, None]
    live = below.astype(jnp.float32).reshape(rows, 1)

    gain_one = wide(ln1_gain)
    gain_two = wide(ln2_gain)
    pairs = local // (2 * HD)
    hidden_halves = halves(hidden_in)
    qkv_own, context_own, lse_own = attend(
        [hidden_in], mask, [w_three], b_qv, pairs, 0, None, "attend_own"
    )
    first_half = attend(
        hidden_halves, mask, qkv_near, cut(b_qv_peer, x, 2, 1), pairs, 0, None, "attend_near"
    )
    qkv_peer, context_peer, lse_peer = attend(
        hidden_halves, mask, qkv_side, cut(b_qv_peer, 1 - x, 2, 1), pairs, pairs // 2, first_half,
        "attend_side",
    )

    def from_peer(here, there):
        return ordered(core == 0, here, there, 1)

    branch = dot_nn(context_own, w_out) + from_peer(*[dot_nn(context_peer, w) for w in w_out_peer])
    normed1, unit_one, scale_one = layer_norm_parts(
        wide(hidden_in) + branch + wide(b_out), gain_one, wide(ln1_bias)
    )
    normed_low = low(normed1)
    normed_halves = halves(normed_low)
    active_own, slope_own = up_and_gelu([normed_low], [w_up], b_up, units, 0, None, "up_own")
    first_half = up_and_gelu(
        normed_halves, up_near, cut(b_up_peer, x, 2, 0), units, 0, None, "up_near"
    )
    active_peer, slope_peer = up_and_gelu(
        normed_halves, up_side, cut(b_up_peer, 1 - x, 2, 0), units, units // 2, first_half, "up_side"
    )
    with jax.named_scope("ffn_out"):
        ffn = dot_nn(active_own, w_down) + from_peer(
            *[dot_nn(active_peer, w) for w in w_down_peer]
        )
    layer_out, unit_two, scale_two = layer_norm_parts(
        normed1 + ffn + wide(b_down), gain_two, wide(ln2_bias)
    )

    def reduce_core(left_own, left_peer, right_halves, product, name):
        here, there = right_halves
        with jax.named_scope(name + "_grads"):
            peer_there = low(product(left_peer, there))
            own_there = low(product(left_own, there))
        peer_far = over_core(peer_there, name + "_peer")
        own_far = over_core(own_there, name + "_own")
        with jax.named_scope(name + "_grads_peer"):
            peer_here = low(product(left_peer, here) + wide(peer_far))
        home = over_y(peer_here, name)
        with jax.named_scope(name + "_grads_own"):
            own = low(product(left_own, here) + wide(own_far))
        return own, home

    def reduce_rest(own, home, unit_axis, axis, name):
        home_mine = lax.slice_in_dim(home, 0, home.shape[unit_axis] // 2, axis=unit_axis)
        home_other = lax.slice_in_dim(
            home, home.shape[unit_axis] // 2, home.shape[unit_axis], axis=unit_axis
        )
        side = over_x(low(wide(cut(own, 1 - x, 2, unit_axis)) + wide(home_other)), name)
        own_mine = cut(own, x, 2, unit_axis)

        def three(half):
            return sum(wide(cut(value, half, 2, axis)) for value in (own_mine, home_mine, side))

        got = over_near(low(three(1 - near)), name)
        kept = low(three(near) + wide(got))
        final = low(wide(kept) + wide(over_far(kept, name)))
        both_near = ordered(near == 0, final, over_near(final, name + "_back"), axis)
        return ordered(x == 0, both_near, over_x(both_near, name + "_back"), unit_axis)

    def finish(mine, axis, name):
        return wide(ordered(core == 0, mine, over_core(mine, name + "_back"), axis))

    out_cot = wide(out_cotangent) * live
    resid2_grad, gain2_grad, bias2_grad = layer_norm_back(out_cot, unit_two, scale_two, gain_two)
    ffn_low = low(resid2_grad)
    ffn_halves = halves(ffn_low)
    down_bias_grad = jnp.sum(wide(ffn_low), axis=0)
    down_own, down_home = reduce_core(active_own, active_peer, ffn_halves, dot_tn, "down")

    def linear_grad(grads, weights, slope):
        total = sum(dot_nt(g, w) for g, w in zip(grads, weights))
        return low(total * wide(slope))

    linear_own = linear_grad([ffn_low], [w_down], slope_own)
    linear_peer = linear_grad(ffn_halves, w_down_peer, slope_peer)

    def flipped(left, right):
        return dot_tn(right, left)

    up_own, up_home = reduce_core(linear_own, linear_peer, normed_halves, flipped, "up")

    def back_up(near_part, side_part):
        half = units // 2
        return dot_nt(linear_peer[:, :half], near_part) + dot_nt(linear_peer[:, half:], side_part)

    normed1_grad = (
        resid2_grad
        + dot_nt(linear_own, w_up)
        + from_peer(*[back_up(a, b) for a, b in zip(up_near, up_side)])
    )
    up_bias_own = jnp.sum(wide(linear_own), axis=0)
    up_bias_peer = jnp.sum(wide(linear_peer), axis=0)
    resid1_grad, gain1_grad, bias1_grad = layer_norm_back(
        normed1_grad, unit_one, scale_one, gain_one
    )
    attn_low = low(resid1_grad)
    attn_halves = halves(attn_low)
    out_bias_grad = jnp.sum(wide(attn_low), axis=0)
    dqkv_own, sums_own = attend_back([attn_low], mask, [w_out], qkv_own, lse_own, "back_own")
    dqkv_peer, sums_peer = attend_back(
        attn_halves, mask, w_out_peer, qkv_peer, lse_peer, "back_peer"
    )

    def four(left, right):
        three, context = left
        rows_part, grad_part = right
        inner = jnp.einsum("cte,td->cde", three, rows_part, preferred_element_type=jnp.float32)
        return jnp.concatenate([inner, dot_tn(grad_part, context)[None]], axis=0)

    rest_own, rest_home = reduce_core(
        (dqkv_own, context_own),
        (dqkv_peer, context_peer),
        list(zip(hidden_halves, attn_halves)),
        four,
        "rest",
    )

    def into_input(grads, weights):
        return jnp.einsum("cte,cde->td", grads, weights, preferred_element_type=jnp.float32)

    def back_input(near_part, side_part):
        half = local // 2
        return into_input(dqkv_peer[:, :, :half], near_part) + into_input(
            dqkv_peer[:, :, half:], side_part
        )

    with jax.named_scope("input_back"):
        input_grad = (
            resid1_grad
            + into_input(dqkv_own, w_three)
            + from_peer(*[back_input(a, b) for a, b in zip(qkv_near, qkv_side)])
        )

    down_grad = finish(reduce_rest(down_own, down_home, 0, 0, "down"), 1, "down")
    up_grad = finish(reduce_rest(up_own, up_home, 1, 0, "up"), 0, "up")
    rest_grad = finish(reduce_rest(rest_own, rest_home, 2, 1, "rest"), 1, "rest")
    qkv_grad = jnp.transpose(rest_grad[:3], (1, 0, 2))
    out_grad = rest_grad[3].T

    def both(own, peer):
        half = peer.shape[-1] // 2
        peer = ordered(x == 0, peer[..., :half], peer[..., half:], peer.ndim - 1)
        return ordered(y == 0, own[None], peer[None], 0).reshape(-1)

    vectors = jnp.concatenate(
        [
            both(jnp.sum(sums_own, axis=0), jnp.sum(sums_peer, axis=0)),
            both(up_bias_own, up_bias_peer),
            out_bias_grad, gain1_grad, bias1_grad, down_bias_grad, gain2_grad, bias2_grad,
        ]
    ).reshape(-1, 128)
    for step in (over_core, over_y, over_x, over_near, over_far):
        vectors = vectors + step(vectors, "vectors")
    flat = vectors.reshape(-1)
    qv_size, up_size = 2 * local, units
    qv_grad = lax.dynamic_slice_in_dim(flat, y * qv_size, qv_size, 0).reshape(2, local)
    up_bias_grad = lax.dynamic_slice_in_dim(flat, 2 * qv_size + y * up_size, up_size, 0)
    singles = flat[2 * qv_size + 2 * up_size :].reshape(6, width)
    return (
        layer_out, input_grad, qkv_grad, qv_grad, out_grad, singles[0], singles[1], singles[2],
        up_grad, up_bias_grad, down_grad, singles[3], singles[4], singles[5],
    )


def local(
    hidden_in,
    lengths,
    key_mask,
    w_qkv,
    b_qv,
    w_out,
    b_out,
    ln1_gain,
    ln1_bias,
    w_up,
    b_up,
    w_down,
    b_down,
    ln2_gain,
    ln2_bias,
    out_cotangent,
):
    rows = hidden_in.shape[0]
    pages = lengths.shape[0]
    local_width = w_qkv.shape[2]
    local_heads = local_width // HD
    factor = float(HD) ** (-0.5)
    group = pages * PAGE
    slots = jnp.arange(PAGE, dtype=jnp.int32)
    valid = (slots[None, :] < lengths[:, None]) & (key_mask == 1)
    row_ids = lax.axis_index("mp") * rows + jnp.arange(rows, dtype=jnp.int32)
    row_page = row_ids // PAGE
    row_slot = row_ids % PAGE
    page_ids = jnp.arange(pages, dtype=jnp.int32)
    row_length = jnp.sum(
        jnp.where(row_page[:, None] == page_ids[None, :], lengths[None, :], 0), axis=1
    )
    row_live = (row_slot < row_length).astype(jnp.float32)
    gain_one = ln1_gain.astype(jnp.float32)
    gain_two = ln2_gain.astype(jnp.float32)
    inputs_all = lax.all_gather(hidden_in, "mp", axis=0, tiled=True)
    bias_rows = jnp.stack([b_qv[0], jnp.zeros_like(b_qv[0]), b_qv[1]]).astype(jnp.float32)
    projected = (
        jnp.einsum("td,dce->tce", inputs_all, w_qkv, preferred_element_type=jnp.float32) + bias_rows
    )
    projected_low = projected.astype(jnp.bfloat16).reshape(pages, PAGE, 3, local_heads, HD)
    query = projected_low[:, :, 0]
    keys = projected_low[:, :, 1]
    values = projected_low[:, :, 2]
    scores = page_scores(query, keys, valid, factor)
    highest = jnp.max(scores, axis=-1, keepdims=True)
    expo = jnp.exp(scores - highest)
    expo_sum = jnp.sum(expo, axis=-1, keepdims=True)
    probs_low = (expo / expo_sum).astype(jnp.bfloat16)
    log_total = highest + jnp.log(expo_sum)
    context = jnp.einsum("phqk,pkhd->pqhd", probs_low, values, preferred_element_type=jnp.float32)
    context_low = context.astype(jnp.bfloat16).reshape(group, local_width)
    attn_rows = lax.psum_scatter(
        jnp.dot(context_low, w_out, preferred_element_type=jnp.float32),
        "mp",
        scatter_dimension=0,
        tiled=True,
    ) + b_out.astype(jnp.float32)
    normed1, unit_one, scale_one = layer_norm_parts(
        hidden_in.astype(jnp.float32) + attn_rows, gain_one, ln1_bias.astype(jnp.float32)
    )
    normed1_low = normed1.astype(jnp.bfloat16)
    normed_all = lax.all_gather(normed1_low, "mp", axis=0, tiled=True)
    up_linear = jnp.dot(normed_all, w_up, preferred_element_type=jnp.float32) + b_up.astype(
        jnp.float32
    )
    up_active = gelu_exact(up_linear).astype(jnp.bfloat16)
    ffn_rows = lax.psum_scatter(
        jnp.dot(up_active, w_down, preferred_element_type=jnp.float32).astype(jnp.bfloat16),
        "mp",
        scatter_dimension=0,
        tiled=True,
    ).astype(jnp.float32) + b_down.astype(jnp.float32)
    layer_out, unit_two, scale_two = layer_norm_parts(
        normed1 + ffn_rows, gain_two, ln2_bias.astype(jnp.float32)
    )
    out_cot = out_cotangent.astype(jnp.float32) * row_live[:, None]
    resid2_grad, gain2_grad, bias2_grad = layer_norm_back(out_cot, unit_two, scale_two, gain_two)
    ffn_grad_low = resid2_grad.astype(jnp.bfloat16)
    down_bias_grad = jnp.sum(ffn_grad_low.astype(jnp.float32), axis=0)
    piece = lax.all_gather(ffn_grad_low, "mp", axis=0, tiled=True)
    down_total = jnp.einsum("tf,td->fd", up_active, piece, preferred_element_type=jnp.float32)
    active_rows = jnp.einsum("td,fd->tf", piece, w_down, preferred_element_type=jnp.float32)
    down_grad = down_total
    gelu_value, gelu_pull = jax.vjp(gelu_exact, up_linear)
    linear_grad_low = gelu_pull(active_rows)[0].astype(jnp.bfloat16)
    up_bias_grad = jnp.sum(linear_grad_low.astype(jnp.float32), axis=0)
    up_grad = jnp.einsum(
        "td,tf->df", normed_all, linear_grad_low, preferred_element_type=jnp.float32
    )
    piece = linear_grad_low
    normed1_grad = resid2_grad + lax.psum_scatter(
        jnp.einsum("tf,df->td", piece, w_up, preferred_element_type=jnp.float32).astype(
            jnp.bfloat16
        ),
        "mp",
        scatter_dimension=0,
        tiled=True,
    ).astype(jnp.float32)
    resid1_grad, gain1_grad, bias1_grad = layer_norm_back(
        normed1_grad, unit_one, scale_one, gain_one
    )
    attn_grad_low = resid1_grad.astype(jnp.bfloat16)
    out_bias_grad = jnp.sum(attn_grad_low.astype(jnp.float32), axis=0)
    piece = lax.all_gather(attn_grad_low, "mp", axis=0, tiled=True)
    out_total = jnp.einsum("te,td->ed", context_low, piece, preferred_element_type=jnp.float32)
    context_rows = jnp.einsum("td,ed->te", piece, w_out, preferred_element_type=jnp.float32)
    out_weight_grad = out_total
    context_grad_low = context_rows.astype(jnp.bfloat16).reshape(pages, PAGE, local_heads, HD)
    scores_again = page_scores(query, keys, valid, factor)
    probs = jnp.exp(scores_again - log_total)
    prob_grad = jnp.einsum(
        "pqhd,pkhd->phqk", context_grad_low, values, preferred_element_type=jnp.float32
    )
    value_grad = jnp.einsum(
        "phqk,pqhd->pkhd", probs_low, context_grad_low, preferred_element_type=jnp.float32
    )
    row_inner = jnp.sum(probs * prob_grad, axis=-1, keepdims=True)
    score_grad_low = (probs * (prob_grad - row_inner)).astype(jnp.bfloat16)
    query_grad = (
        jnp.einsum("phqk,pkhd->pqhd", score_grad_low, keys, preferred_element_type=jnp.float32)
        * factor
    )
    key_grad = (
        jnp.einsum("phqk,pqhd->pkhd", score_grad_low, query, preferred_element_type=jnp.float32)
        * factor
    )
    projected_grad_low = (
        jnp.stack([query_grad, key_grad, value_grad], axis=2)
        .astype(jnp.bfloat16)
        .reshape(group, 3, local_width)
    )
    qkv_weight_grad = jnp.einsum(
        "td,tce->dce", inputs_all, projected_grad_low, preferred_element_type=jnp.float32
    )
    projected_sums = jnp.sum(projected_grad_low.astype(jnp.float32), axis=0)
    qkv_bias_grad = jnp.stack([projected_sums[0], projected_sums[2]])
    piece = projected_grad_low
    input_grad = resid1_grad + lax.psum_scatter(
        jnp.einsum("tce,dce->td", piece, w_qkv, preferred_element_type=jnp.float32).astype(
            jnp.bfloat16
        ),
        "mp",
        scatter_dimension=0,
        tiled=True,
    ).astype(jnp.float32)
    qkv_weight_grad, qkv_bias_grad, out_weight_grad, up_grad, up_bias_grad, down_grad = (
        lax.psum(qkv_weight_grad.astype(jnp.bfloat16), "dp").astype(jnp.float32),
        lax.psum(qkv_bias_grad.astype(jnp.bfloat16), "dp").astype(jnp.float32),
        lax.psum(out_weight_grad.astype(jnp.bfloat16), "dp").astype(jnp.float32),
        lax.psum(up_grad.astype(jnp.bfloat16), "dp").astype(jnp.float32),
        lax.psum(up_bias_grad.astype(jnp.bfloat16), "dp").astype(jnp.float32),
        lax.psum(down_grad.astype(jnp.bfloat16), "dp").astype(jnp.float32),
    )
    out_bias_grad, gain1_grad, bias1_grad, down_bias_grad, gain2_grad, bias2_grad = lax.psum(
        (out_bias_grad, gain1_grad, bias1_grad, down_bias_grad, gain2_grad, bias2_grad),
        ("dp", "mp"),
    )
    return (
        layer_out,
        input_grad,
        qkv_weight_grad,
        qkv_bias_grad,
        out_weight_grad,
        out_bias_grad,
        gain1_grad,
        bias1_grad,
        up_grad,
        up_bias_grad,
        down_grad,
        down_bias_grad,
        gain2_grad,
        bias2_grad,
    )


def solution(mesh):
    dp, mp = mesh.shape["dp"], mesh.shape["mp"]

    def body(hidden_in, *rest):
        if hidden_in.shape[0] % PAGE == 0 and mp == 2 and dp == 16:
            return paged(hidden_in, *rest, dp)
        return local(hidden_in, *rest)

    return jax.shard_map(
        body,
        mesh=mesh,
        in_specs=(
            P(("dp", "mp"), None),
            P("dp"),
            P("dp", None),
            P(None, None, "mp"),
            P(None, "mp"),
            P("mp", None),
            P(),
            P(),
            P(),
            P(None, "mp"),
            P("mp"),
            P("mp", None),
            P(),
            P(),
            P(),
            P(("dp", "mp"), None),
        ),
        out_specs=(
            P(("dp", "mp"), None),
            P(("dp", "mp"), None),
            P(None, None, "mp"),
            P(None, "mp"),
            P("mp", None),
            P(),
            P(),
            P(),
            P(None, "mp"),
            P("mp"),
            P("mp", None),
            P(),
            P(),
            P(),
        ),
        check_vma=False,
    )
```
